128 devices in a mesh: parts: 128 (over y, z, x, core).
Axes of the slice: x: 4, y: 4, z: 4, core: 2. Of those that a mesh axis runs over, the one named last changes fastest.
Arguments:
- a_cols: int32 [4096, 7], replicated, may hold values from 0 to 4095, as said below
- p_col: int32 [4096], replicated, may hold values from 0 to 255, as said below
- coarse_cols: int32 [256, 14], replicated, may hold values from 0 to 255, as said below
- a_vals: bfloat16 [4096, 7, 192, 192], P('parts'), may hold values from -0.15625 to 0.15625
- p_vals: bfloat16 [4096, 192, 192], P('parts'), may hold values from -0.5 to 0.5
Outputs:
- coarse: float32 [256, 14, 192, 192], P('parts')
The draws below stay inside these ranges and needn't reach their ends.
Inputs may be any that keep to these rules, and one draw needn't show every extreme that they name: `a_cols`: regions are numbered 0 to 127; fine row i lies in region g = i // 32 with local index l = i % 32; o is the list 0, 1, -1, 4, -4, 16, -16 and region g + o(s) is taken cyclically. Slot 0 of row i holds i. For l < 6, slot l + 1 holds the row of region g + o(l + 1) whose local index is q - 1, where q is the slot whose offset is the negative of o(l + 1), and the other slots hold rows of region g with local index 6 or more. For l >= 6 slots 1 to 6 hold rows of region g. For fine row i of region g with local index l: if l < 6, p_col[i] is a coarse row of region g + o(l + 1), else of region g; coarse row r belongs to region r // 2. `coarse_cols`: row r of region g lists, in an order of its own, the 2 coarse rows of each of the regions g + o(s), s = 0 to 6.
All inputs are finite; a program needn't handle non-finite values.
Results may differ from the reference program's by a relative error of at most 0.0029.
Values may be sent and summed in bfloat16 or wider, within the bound.
No kernel may reach another device: no remote copies, remote signals or barrier semaphores. Data moves between devices by JAX's collectives and lax.ppermute only.
A program may use at most 256 MiB of HBM per device.

```python
import jax
import jax.numpy as jnp
from jax import lax

B = 192
C = 192
KA = 7
RC = 2
RF = 32
NF = 4096
NC = 256
KC = 14


OFFSETS = [0, 1, -1, 4, -4, 16, -16]


OPPOSITE = [0, 2, 1, 4, 3, 6, 5]


def draw_a_cols(key, part):
    regions = NF // RF
    fine_rows = jnp.arange(NF, dtype=jnp.int32)
    region_of = fine_rows // RF
    local_row = fine_rows % RF
    key_any, key_inner = jax.random.split(key)
    any_rows = jax.random.randint(key_any, (NF, KA), 0, RF, dtype=jnp.int32)
    inner_rows = jax.random.randint(key_inner, (NF, KA), 6, RF, dtype=jnp.int32)
    slot_ids = jnp.arange(KA, dtype=jnp.int32)[None, :]
    offsets = jnp.array(OFFSETS, dtype=jnp.int32)
    opposite = jnp.array(OPPOSITE, dtype=jnp.int32)
    neighbour = (region_of[:, None] + offsets[None, :]) % regions * RF + (opposite[None, :] - 1)
    own_pick = region_of[:, None] * RF + jnp.where(local_row[:, None] < 6, inner_rows, any_rows)
    columns = jnp.where(slot_ids == 0, fine_rows[:, None], jnp.where(local_row[:, None] == slot_ids - 1, neighbour, own_pick))
    return columns.astype(jnp.int32)


def draw_p_col(key, part):
    regions = NF // RF
    fine_rows = jnp.arange(NF, dtype=jnp.int32)
    region_of = fine_rows // RF
    local_row = fine_rows % RF
    offsets = jnp.array(OFFSETS, dtype=jnp.int32)
    choose = jax.random.randint(key, (NF,), 0, RC, dtype=jnp.int32)
    shift_by = jnp.where(local_row < 6, offsets[jnp.minimum(local_row + 1, 6)], 0)
    return ((region_of + shift_by) % regions * RC + choose).astype(jnp.int32)


def draw_coarse_cols(key, part):
    regions = NC // RC
    coarse_rows = jnp.arange(NC, dtype=jnp.int32)
    region_of = coarse_rows // RC
    slot_ids = jnp.arange(KC, dtype=jnp.int32)
    offsets = jnp.array(OFFSETS, dtype=jnp.int32)
    base = (region_of[:, None] + offsets[slot_ids // RC][None, :]) % regions * RC + (slot_ids % RC)[None, :]
    orders = jax.vmap(lambda row_key: jax.random.permutation(row_key, KC))(jax.random.split(key, NC))
    return jnp.take_along_axis(base, orders.astype(jnp.int32), axis=1).astype(jnp.int32)


def shard_levels(own_key, shape, pieces, smallest, top_value):
    loudness = 1.0
    for position, shards_of in pieces:
        draws = jax.random.uniform(jax.random.fold_in(jax.random.fold_in(own_key, 6), position), (shards_of,), jnp.float32, smallest / len(pieces), top_value / len(pieces))
        loudness = loudness * jnp.repeat(jnp.exp(draws), shape[position] // shards_of).reshape((-1,) + (1,) * (len(shape) - 1 - position))
    return loudness


def scatter_about(rng, extent, width, most, cuts=(), kind=jnp.bfloat16):
    drawn = jax.random.normal(rng, extent, jnp.float32) * width
    if len(cuts) > 0:
        drawn = shard_levels(rng, extent, cuts, -0.22, 0.18) * drawn
    return jnp.clip(drawn, min=-most, max=most).astype(kind)


def setup_inputs(seed: int = 0) -> dict:
    key_of = jax.random.split(jax.random.key(seed), 6)
    return {
        "a_cols": draw_a_cols(jax.random.fold_in(key_of[5], 71), 0),
        "p_col": draw_p_col(jax.random.fold_in(key_of[5], 71), 0),
        "coarse_cols": draw_coarse_cols(jax.random.fold_in(key_of[5], 71), 0),
        "a_vals": scatter_about(key_of[3], (NF, KA, B, B), (KA * B) ** -0.5, 0.15625, ((0, 128),)),
        "p_vals": scatter_about(key_of[4], (NF, B, C), 128 ** -0.5, 0.5, ((0, 128),)),
    }


def reference(a_cols, p_col, coarse_cols, a_vals, p_vals):
    regions = NF // RF

    def region_step(region_id, accumulated):
        first_row = (jnp.asarray(region_id) * RF).astype(jnp.int32)
        columns = lax.dynamic_slice_in_dim(a_cols, first_row, RF, 0)
        blocks = lax.dynamic_slice_in_dim(a_vals, first_row, RF, 0).astype(jnp.float32)
        own_prolong = lax.dynamic_slice_in_dim(p_vals, first_row, RF, 0).astype(jnp.float32)
        gathered = p_vals[columns].astype(jnp.float32)
        products = jnp.einsum('ikab,ikbc->ikac', blocks, gathered).astype(jnp.bfloat16)
        galerkin = jnp.einsum('iba,ikbc->ikac', own_prolong, products.astype(jnp.float32))
        targets = p_col[columns]
        coarse_rows = lax.dynamic_slice_in_dim(p_col, first_row, RF, 0)
        listed = coarse_cols[coarse_rows]
        equal_slots = listed[:, None, :] == targets[:, :, None]
        first_slot = equal_slots & (jnp.cumsum(equal_slots.astype(jnp.int32), axis=2) == 1)
        placed = jnp.einsum('ikm,ikab->imab', first_slot.astype(jnp.float32), galerkin,
                            precision=lax.Precision.HIGHEST)
        return accumulated.at[coarse_rows].add(placed)

    return lax.fori_loop(0, regions, region_step, jnp.zeros((NC, KC, C, C), jnp.float32))
```

```python
import jax
import jax.numpy as jnp
from jax import lax
from jax.experimental import pallas as pl
from jax.experimental.pallas import tpu as pltpu
from jax.sharding import PartitionSpec as P

OFFSETS = [0, 1, -1, 4, -4, 16, -16]
OPPOSITE = [0, 2, 1, 4, 3, 6, 5]
B = 192
RF = 32
RC = 2
KA = 7
KC = 14
FACES = 6
INNER = RF - FACES
REGIONS = 128
WINDOW = 128
ROWS = 2
F32 = jnp.float32
BF16 = jnp.bfloat16
MIB = 1024 * 1024


def dot(a, b):
    return lax.dot_general(a, b, (((1,), (0,)), ((), ())), preferred_element_type=F32)


def link_pairs(link):
    if link == 0:
        return [(d, d ^ 1) for d in range(REGIONS)]
    if link == 1:
        return [(d, (d + 1 if d % 2 else d - 1) % REGIONS) for d in range(REGIONS)]
    return [(d, (d + OFFSETS[link + 1]) % REGIONS) for d in range(REGIONS)]


def sent_face(link, core):
    return (1 + core, 2 - core)[link] if link < 2 else link + 1


def received_face(link, core):
    return (2 - core, 1 + core)[link] if link < 2 else link + 1


def sender_of(link, region, core):
    if link < 2:
        step = 1 - 2 * core if link == 0 else 2 * core - 1
    else:
        step = -OFFSETS[link + 1]
    return (region + step + REGIONS) % REGIONS


def mate_row(link, face):
    return 2 - face if link < 2 else OPPOSITE[face] - 1


def fill_slots(slot_ref, list_ref, region):
    for r in range(RC):
        for m in reversed(range(KC)):
            slot_ref[r, list_ref[m, region * RC + r]] = m


def face_kernel(region_ref, cols_ref, pcol_ref, a_hbm, p_hbm, o0, o1, o2, o3, o4, o5,
                a_ref, p_ref, sums_ref, rhs_ref, a_sem, p_sem):
    outs = (o0, o1, o2, o3, o4, o5)
    region = region_ref[0]
    core = region % 2
    first_row = region * RF
    base = first_row % WINDOW
    a_copies = [pltpu.make_async_copy(a_hbm.at[i], a_ref.at[i], a_sem.at[i]) for i in range(FACES)]
    p_copies = [pltpu.make_async_copy(p_hbm.at[pl.ds(8 * i, 8)], p_ref.at[pl.ds(8 * i, 8)], p_sem.at[i]) for i in range(4)]
    for c in p_copies:
        c.start()
    for c in a_copies:
        c.start()
    for c in p_copies:
        c.wait()
    for link in range(FACES):
        if link == 0:
            a_copies[0].wait()
            a_copies[1].wait()
        elif link > 1:
            a_copies[link].wait()
        face = sent_face(link, core)
        row = face - 1
        p_own = p_ref[row]
        sums_ref[...] = jnp.zeros_like(sums_ref)
        for k in range(1, KA - 1):
            slot = k + (k >= face) if link > 1 else k + (k >= face).astype(jnp.int32)
            column = cols_ref[slot, base + row]
            which = pcol_ref[column] - region * RC
            sums_ref[which] += dot(a_ref[row, slot], p_ref[column - first_row])
        rhs_ref[:, 0:B] = dot(a_ref[row, 0], p_own).astype(BF16)
        rhs_ref[:, B : 2 * B] = sums_ref[0].astype(BF16)
        rhs_ref[:, 2 * B : 3 * B] = sums_ref[1].astype(BF16)
        rhs_ref[:, 3 * B : 4 * B] = a_ref[row, face]
        outs[link][...] = dot(p_own.T, rhs_ref[...]).astype(BF16)


def inner_kernel(region_ref, cols_ref, pcol_ref, list_ref, a_ref, p_ref, out_ref, slot_ref):
    region = region_ref[0]
    first_row = region * RF
    base = first_row % WINDOW
    out_ref[...] = jnp.zeros_like(out_ref)
    fill_slots(slot_ref, list_ref, region)

    def step(i, carry):
        for s in range(ROWS):
            row = i * ROWS + s + FACES
            p_turned = p_ref[row].T
            r = pcol_ref[first_row + row] - region * RC
            columns = [cols_ref[k, base + row] for k in range(KA)]
            products = [dot(a_ref[row, k], p_ref[columns[k] - first_row]).astype(BF16) for k in range(KA)]
            for k in range(KA):
                out_ref[r, slot_ref[r, pcol_ref[columns[k]]]] += dot(p_turned, products[k])
        return carry

    lax.fori_loop(0, INNER // ROWS, step, 0)


def merge_kernel(region_ref, pcol_ref, list_ref, p_ref, m0, m1, m2, m3, m4, m5, acc_ref, out_hbm,
                 buf_ref, diag_ref, slot_ref, out_sem, rest_sem, diag_sem, cross_sem):
    msgs = (m0, m1, m2, m3, m4, m5)
    region = region_ref[0]
    core = region % 2
    first_row = region * RF
    fill_slots(slot_ref, list_ref, region)
    copies = []

    def send(source, r, m, sem):
        c = pltpu.make_async_copy(source, out_hbm.at[r, m], sem)
        c.start()
        copies.append(c)

    places = []
    for link in range(FACES):
        face = received_face(link, core)
        sender = sender_of(link, region, core)
        r = pcol_ref[sender * RF + face - 1] - region * RC
        mate = mate_row(link, face)
        which = pcol_ref[first_row + mate] - sender * RC
        spots = [slot_ref[r, sender * RC + h] for h in range(2)]
        places.append((r, spots, mate, which))
        for h in range(2):
            m = slot_ref[1 - r, sender * RC + h]
            send(acc_ref.at[1 - r, m], 1 - r, m, rest_sem.at[link, h])
    diag = [slot_ref[r, region * RC + r] for r in range(RC)]
    for r in range(RC):
        m = slot_ref[r, region * RC + 1 - r]
        send(acc_ref.at[r, m], r, m, cross_sem.at[r])
        diag_ref[r] = acc_ref[r, diag[r]]
    for link in range(FACES):
        r, spots, mate, which = places[link]
        msg = msgs[link]
        diag_ref[r] += msg[:, 0:B].astype(F32)
        for h in range(2):
            buf_ref[link, h] = acc_ref[r, spots[h]] + msg[:, (h + 1) * B : (h + 2) * B].astype(F32)
        buf_ref[link, which] += dot(msg[:, 3 * B : 4 * B], p_ref[mate])
        for h in range(2):
            send(buf_ref.at[link, h], r, spots[h], out_sem.at[link, h])
    for r in range(RC):
        send(diag_ref.at[r], r, diag[r], diag_sem.at[r])
    for c in copies:
        c.wait()


SMEM_ALL = pl.BlockSpec(memory_space=pltpu.SMEM)
VMEM_ALL = pl.BlockSpec(memory_space=pltpu.VMEM)
ANY_ALL = pl.BlockSpec(memory_space=pl.ANY)
COLS = pl.BlockSpec((KA, WINDOW), lambda i, g: (0, g[0] * RF // WINDOW), memory_space=pltpu.SMEM)
DMA = pltpu.SemaphoreType.DMA
SLOTS = pltpu.SMEM((RC, REGIONS * RC), jnp.int32)


def in_vmem(x):
    return pltpu.with_memory_space_constraint(x, pltpu.VMEM)


def in_hbm(x):
    return pltpu.with_memory_space_constraint(x, pltpu.HBM)


def per_device(a_cols, p_col, coarse_cols, a_vals, p_vals):
    region = lax.axis_index("parts").astype(jnp.int32).reshape(1)
    cols = a_cols.T
    listed = coarse_cols.T
    messages = pl.pallas_call(
        face_kernel,
        grid_spec=pltpu.PrefetchScalarGridSpec(
            num_scalar_prefetch=1,
            grid=(1,),
            in_specs=[COLS, SMEM_ALL, ANY_ALL, ANY_ALL],
            out_specs=[VMEM_ALL] * FACES,
            scratch_shapes=[
                pltpu.VMEM((FACES, KA, B, B), BF16),
                pltpu.VMEM((RF, B, B), BF16),
                pltpu.VMEM((2, B, B), F32),
                pltpu.VMEM((B, 4 * B), BF16),
                DMA((FACES,)),
                DMA((4,)),
            ],
        ),
        out_shape=[pltpu.VMEM((B, 4 * B), BF16)] * FACES,
        compiler_params=pltpu.CompilerParams(vmem_limit_bytes=14 * MIB),
        name="faces",
    )(region, cols, p_col, in_hbm(a_vals), in_hbm(p_vals))
    received = [None] * FACES
    for link in (0, 2, 3, 4, 5, 1):
        message = messages[link]
        if link == 1:
            message, received[0] = lax.optimization_barrier((message, received[0]))
        received[link] = lax.ppermute(message, "parts", link_pairs(link))
    inner = pl.pallas_call(
        inner_kernel,
        grid_spec=pltpu.PrefetchScalarGridSpec(
            num_scalar_prefetch=1,
            grid=(1,),
            in_specs=[COLS, SMEM_ALL, SMEM_ALL, VMEM_ALL, VMEM_ALL],
            out_specs=VMEM_ALL,
            scratch_shapes=[SLOTS],
        ),
        out_shape=pltpu.VMEM((RC, KC, B, B), F32),
        compiler_params=pltpu.CompilerParams(vmem_limit_bytes=4 * MIB),
        name="inner",
    )(region, cols, p_col, listed, in_vmem(a_vals), in_vmem(p_vals))
    return pl.pallas_call(
        merge_kernel,
        in_specs=[SMEM_ALL, SMEM_ALL, SMEM_ALL] + [VMEM_ALL] * 8,
        out_specs=ANY_ALL,
        out_shape=jax.ShapeDtypeStruct((RC, KC, B, B), F32),
        scratch_shapes=[
            pltpu.VMEM((FACES, 2, B, B), F32),
            pltpu.VMEM((RC, B, B), F32),
            SLOTS,
            DMA((FACES, 2)),
            DMA((FACES, 2)),
            DMA((RC,)),
            DMA((RC,)),
        ],
        compiler_params=pltpu.CompilerParams(vmem_limit_bytes=12 * MIB),
        name="merge",
    )(region, p_col, listed, in_vmem(p_vals), *[in_vmem(x) for x in received], in_vmem(inner))


def solution(mesh):
    placed = (P(), P(), P(), P("parts", None, None, None), P("parts", None, None))
    return jax.shard_map(
        per_device,
        mesh=mesh,
        in_specs=placed,
        out_specs=P("parts", None, None, None),
        check_vma=False,
    )
```
